512 devices in a mesh: blk: 32 (over y, x, core), mpo: 16 (over z).
Axes of the slice: x: 4, y: 4, z: 16, core: 2. Of those that a mesh axis runs over, the one named last changes fastest.
Arguments:
- theta: float32 [64, 128, 16, 128], P('blk'), may hold values from -6 to 6
- block_dims: int32 [64, 2], P('blk'), may hold values from 32 to 128, as said below
- pair_mask: int32 [96, 64], P(None, 'blk'), may hold values 0 or 1
- term_charge: int32 [96], replicated, may hold values from -1 to 1
- left_env: float32 [96, 64, 128, 128], P('mpo', 'blk'), may hold values from -0.5 to 0.5
- right_env: float32 [96, 64, 128, 128], P('mpo', 'blk'), may hold values from -0.5 to 0.5
- site_one: float32 [96, 4, 4], replicated, may hold values from -0.3125 to 0.3125
- site_two: float32 [96, 4, 4], replicated, may hold values from -3 to 3
Outputs:
- hpsi: float32 [64, 128, 16, 128], P('blk', 'mpo')
The draws below stay inside these ranges and needn't reach their ends.
Inputs may be any that keep to these rules, and one draw needn't show every extreme that they name: `block_dims`: kept dimensions of each sector; rows and columns of a block beyond them are empty. The first sector keeps 128 on both sides.
All inputs are finite; a program needn't handle non-finite values. No bound on the sum of `pair_mask` on one device may be relied on, other than what follows from the above.
Results may differ from the reference program's by a relative error of at most 0.0003.
Values sent between devices are 32-bit elements; how exact they have to be, the bound alone decides.
A program may use at most 64 MiB of HBM per device.

```python
import jax
import jax.numpy as jnp
from jax import lax

BOND_CAP = 128
SITE = 4
NSEC = 64
NTERM = 96


def draw_block_dims(key, part):
    values = jax.random.randint(key, (NSEC, 2), BOND_CAP // 4, BOND_CAP + 1)
    leading = jnp.arange(NSEC)[:, None] == 0
    return jnp.where(leading, BOND_CAP, values).astype(jnp.int32)


def with_ends(values, own_key, least, high):
    longest = values.shape.index(max(values.shape))
    spots = []
    for shift in (0, 1):
        where = [jax.random.randint(jax.random.fold_in(own_key, axis), (), 0, length) for axis, length in enumerate(values.shape)]
        where[longest] = (where[longest] + shift) % values.shape[longest]
        spots.append(tuple(where))
    return values.at[spots[0]].set(least).at[spots[1]].set(high)


def shard_levels(stream_key, shape, split, low, largest):
    def one(position, blocks):
        heights = jax.random.uniform(jax.random.fold_in(jax.random.fold_in(stream_key, 6), position), (blocks,), jnp.float32, low / len(split), largest / len(split))
        return jnp.repeat(jnp.exp(heights), shape[position] // blocks).reshape((-1,) + (1,) * (len(shape) - position - 1))

    gain = one(*split[0])
    for cut in split[1:]:
        gain = gain * one(*cut)
    return gain


def scatter_about(key, extent, spread, bound, cuts=(), kind=jnp.bfloat16):
    array = spread * jax.random.normal(key, extent, jnp.float32)
    if cuts:
        array = array * shard_levels(key, extent, cuts, -0.22, 0.18)
    return jnp.clip(array, -bound, bound).astype(kind)


def setup_inputs(seed: int = 0) -> dict:
    streams_of = jax.random.split(jax.random.key(seed), 9)
    return {
        "theta": scatter_about(streams_of[0], (NSEC, BOND_CAP, SITE * SITE, BOND_CAP), 1.0, 6.0, ((0, 32),), jnp.float32),
        "block_dims": draw_block_dims(jax.random.fold_in(streams_of[8], 71), 0),
        "pair_mask": with_ends((jax.random.randint(streams_of[2], (NTERM, NSEC), 0, 4) < 3).astype(jnp.int32), jax.random.fold_in(streams_of[2], 1), 0, 1),
        "term_charge": with_ends(jax.random.randint(streams_of[3], (NTERM,), -1, 2), jax.random.fold_in(streams_of[3], 1), -1, 1).astype(jnp.int32),
        "left_env": scatter_about(streams_of[4], (NTERM, NSEC, BOND_CAP, BOND_CAP), BOND_CAP ** -0.5, 0.5, ((0, 16), (1, 32)), jnp.float32),
        "right_env": scatter_about(streams_of[5], (NTERM, NSEC, BOND_CAP, BOND_CAP), BOND_CAP ** -0.5, 0.5, ((0, 16), (1, 32)), jnp.float32),
        "site_one": scatter_about(streams_of[6], (NTERM, SITE, SITE), (SITE * NTERM) ** -0.5, 0.3125, (), jnp.float32),
        "site_two": scatter_about(streams_of[7], (NTERM, SITE, SITE), SITE ** -0.5, 3.0, (), jnp.float32),
    }


def sector_mask(block_dims, bond_cap):
    positions = jnp.arange(bond_cap, dtype=jnp.int32)
    left_ok = positions[None, :] < block_dims[:, 0:1]
    right_ok = positions[None, :] < block_dims[:, 1:2]
    return (left_ok[:, :, None] & right_ok[:, None, :]).astype(jnp.float32)


def reference(theta, block_dims, pair_mask, term_charge, left_env, right_env, site_one, site_two):
    block_mask = sector_mask(block_dims, BOND_CAP)
    masked = theta * block_mask[:, :, None, :]
    padded = jnp.pad(masked, ((1, 1), (0, 0), (0, 0), (0, 0)))
    highest = lax.Precision.HIGHEST

    def step(summed, items):
        left_block, right_block, first_op, second_op, charge, allowed = items
        start = (1 - charge).astype(jnp.int32)
        source = lax.dynamic_slice_in_dim(padded, start, NSEC, 0)
        site_pair = (first_op[:, None, :, None] * second_op[None, :, None, :]).reshape(SITE * SITE, SITE * SITE)
        moved = jnp.einsum('kac,kcx->kax', left_block, source.reshape(NSEC, BOND_CAP, SITE * SITE * BOND_CAP), precision=highest)
        moved = moved.reshape(NSEC, BOND_CAP, SITE * SITE, BOND_CAP)
        mixed = jnp.einsum('pq,kaqd->kapd', site_pair, moved, precision=highest)
        result = jnp.einsum('kapd,kbd->kapb', mixed, right_block, precision=highest)
        return summed + allowed.astype(summed.dtype)[:, None, None, None] * result, None

    start_sum = jnp.zeros((NSEC, BOND_CAP, SITE * SITE, BOND_CAP), jnp.float32)
    summed, unused = lax.scan(step, start_sum, (left_env, right_env, site_one, site_two, term_charge, pair_mask))
    return summed * block_mask[:, :, None, :]
```

```python
import functools

import jax
import jax.numpy as jnp
from jax import lax
from jax.experimental import pallas as pl
from jax.experimental.pallas import tpu as pltpu
from jax.sharding import PartitionSpec as P

MESH = pl.DeviceIdType.MESH
F32 = jnp.float32
BF16 = jnp.bfloat16
CB = 32


def halves(x):
    high = x.astype(BF16)
    return high, (x - high.astype(F32)).astype(BF16)


def kernel(
    theta, left, right, dims_v, dims_s, charge, pair, one, two,
    out,
    theta_v, halo_v, left_v, right_v, dims_halo, dims_all, split, mixed, rows, part, arrived,
    local_sem, halo_send, halo_recv, ring_send, ring_recv,
):
    terms, _, cap, _ = left.shape
    site = one.shape[1]
    pairs = site * site
    n_blk, n = lax.axis_size("blk"), lax.axis_size("mpo")
    half = n // 2
    rc = cap // n
    blk, me = lax.axis_index("blk"), lax.axis_index("mpo")
    next_blk, last_blk = lax.rem(blk + 1, n_blk), lax.rem(blk + n_blk - 1, n_blk)
    up, down = lax.rem(me + 1, n), lax.rem(me + n - 1, n)
    w0 = me * terms

    local = [
        pltpu.make_async_copy(theta, theta_v, local_sem.at[0]),
        pltpu.make_async_copy(left, left_v, local_sem.at[1]),
        pltpu.make_async_copy(right, right_v, local_sem.at[2]),
    ]
    for copy in local:
        copy.start()

    barrier = pltpu.get_barrier_semaphore()
    for target in ({"blk": next_blk}, {"blk": last_blk}, {"mpo": up}, {"mpo": down}):
        pl.semaphore_signal(barrier, inc=1, device_id=target, device_id_type=MESH)
    pl.semaphore_wait(barrier, 4)

    def halo_copy(side, src, dst, index):
        return pltpu.make_async_remote_copy(
            src_ref=src.at[1 - side], dst_ref=dst.at[side],
            send_sem=halo_send.at[index, side], recv_sem=halo_recv.at[index, side],
            device_id={"blk": next_blk if side == 0 else last_blk}, device_id_type=MESH,
        )

    halo = [halo_copy(side, dims_v, dims_halo, 0) for side in (0, 1)]
    halo += [halo_copy(side, theta, halo_v, 1) for side in (0, 1)]
    for copy in halo:
        copy.start()

    def prepare(source, block_ref, index):
        def body(cb, carry):
            for q in range(pairs):
                start = cb * (CB * pairs) + q
                high, low = halves(block_ref[index, pl.ds(start, CB, stride=pairs), :])
                split[source, cb, pl.ds(q * CB, CB), pl.ds(0, cap)] = high
                split[source, cb, pl.ds(q * CB, CB), pl.ds(cap, cap)] = low
            return carry

        lax.fori_loop(0, cap // CB, body, 0)

    lane = lax.broadcasted_iota(jnp.int32, (8, cap), 1).astype(F32)[0:1]

    def apply_right(slot, w, k, source):
        row = dims_all[source]
        weight = jnp.where(lane < row[1:2], right_v[w, k], 0.0)
        high, low = halves(weight)
        weights = jnp.concatenate(
            [
                jnp.concatenate([high, high], axis=1),
                jnp.concatenate([low, jnp.zeros_like(low)], axis=1),
            ],
            axis=0,
        )
        allowed = pair[w0 + w, k].astype(F32)
        first = [[one[w0 + w, s, t] * allowed for t in range(site)] for s in range(site)]
        second = [[two[w0 + w, u, v] for v in range(site)] for u in range(site)]
        def step(cb, carry):
            both = lax.dot_general(
                split[source, cb], weights, (((1,), (1,)), ((), ())), preferred_element_type=F32
            )
            y = both[:, :cap] + both[:, cap:]
            y = [y[q * CB:(q + 1) * CB] for q in range(pairs)]
            z = [
                [sum(second[u][v] * y[t * site + v] for v in range(site)) for u in range(site)]
                for t in range(site)
            ]
            for s in range(site):
                for u in range(site):
                    p = s * site + u
                    m_high, m_low = halves(sum(first[s][t] * z[t][u] for t in range(site)))
                    start = pl.multiple_of(cb * CB, CB)
                    mixed[slot, pl.ds(start, CB), pl.ds(p * cap, cap)] = m_high
                    mixed[slot, pl.ds(cap + start, CB), pl.ds(p * cap, cap)] = m_low
            return carry

        lax.fori_loop(0, cap // CB, step, 0)

    local[0].wait()
    local[2].wait()
    dims_all[1] = dims_v[0]
    dims_all[2] = dims_v[1]
    for k in range(2):
        prepare(1 + k, theta_v, k)

    def near(w, carry):
        q = charge[w0 + w]
        k = jnp.where(q == 1, 1, 0)
        apply_right(w, w, k, k + 1 - q)
        return carry

    lax.fori_loop(0, terms, near, 0)

    for copy in halo:
        copy.wait()
    for side, source in ((0, 0), (1, 3)):
        outside = blk == (0 if side == 0 else n_blk - 1)
        dims_all[source] = dims_halo[side] * jnp.where(outside, 0.0, 1.0)
        prepare(source, halo_v, side)

    def far(w, carry):
        q = charge[w0 + w]
        k = jnp.where(q == 1, 0, 1)
        apply_right(terms + w, w, k, k + 1 - q)
        return carry

    lax.fori_loop(0, terms, far, 0)

    local[1].wait()

    def rotate(g, carry):
        ahead = pl.multiple_of(lax.rem(me + half - g, n) * rc, rc)
        behind = pl.multiple_of(jnp.where(g == 0, me, lax.rem(me + n - half + g, n)) * rc, rc)
        for w in range(terms):
            q = charge[w0 + w]
            for k in range(2):
                row = dims_all[k + 1 - q]
                block = jnp.concatenate(
                    [left_v[w, k, pl.ds(ahead, rc), :], left_v[w, k, pl.ds(behind, rc), :]], axis=0
                )
                high, low = halves(jnp.where(lane < row[0:1], block, 0.0))
                rows[g, k, w] = jnp.concatenate(
                    [
                        jnp.concatenate([high, high], axis=1),
                        jnp.concatenate([low, jnp.zeros_like(low)], axis=1),
                    ],
                    axis=0,
                )
        return carry

    lax.fori_loop(0, half, rotate, 0)

    wide = 4 * cap

    def compute(g):
        for k in range(2):

            def columns(c, carry):
                start = pl.multiple_of(c * wide, wide)
                total = jnp.zeros((4 * rc, wide), F32)
                for w in range(terms):
                    q = charge[w0 + w]
                    slot = w + jnp.where((q == 1) == (k == 1), 0, terms)
                    total += jnp.dot(
                        rows[g, k, w], mixed[slot, :, pl.ds(start, wide)], preferred_element_type=F32
                    )
                total = total[:2 * rc] + total[2 * rc:]
                part[g, 0, k, :, pl.ds(start, wide)] = total[:rc]
                part[g, 1, k, :, pl.ds(start, wide)] = total[rc:]
                return carry

            lax.fori_loop(0, pairs * cap // wide, columns, 0)

    def ring_copy(step, way, k):
        return pltpu.make_async_remote_copy(
            src_ref=part.at[step, 0 if isinstance(step, int) and step == 0 else way, k], dst_ref=arrived.at[step, way, k],
            send_sem=ring_send.at[step, way, k], recv_sem=ring_recv.at[step, way, k],
            device_id={"mpo": up if way == 0 else down}, device_id_type=MESH,
        )

    def ring_step(step, first):
        for k in range(2):
            for way in range(2):
                if first and k != way:
                    ring_copy(step, way, k).start()
        for k in range(2):
            for way in range(2):
                if not first or k == way:
                    ring_copy(step - 1, way, k).wait_recv()
                    part[step, way, k] += arrived[step - 1, way, k]
                    ring_copy(step, way, k).start()

    compute(0)
    for way in range(2):
        ring_copy(0, way, way).start()
    compute(1)
    ring_step(1, True)

    def later(step, carry):
        compute(step)
        ring_step(step, False)
        return carry

    lax.fori_loop(2, half, later, 0)

    for k in range(2):
        total = part[0, 1, k]
        for way in range(2):
            ring_copy(half - 1, way, k).wait_recv()
            total = total + arrived[half - 1, way, k]
        row = lax.broadcasted_iota(jnp.int32, (rc, cap), 0) + me * rc
        column = lax.broadcasted_iota(jnp.int32, (rc, cap), 1)
        keep = (row < dims_s[k, 0]) & (column < dims_s[k, 1])
        for p in range(pairs):
            out[k, :, p, :] = jnp.where(keep, total[:, p * cap:(p + 1) * cap], 0.0)

    for way in range(2):
        ring_copy(0, way, way).wait_send()

    def drain(step, carry):
        for way in range(2):
            for k in range(2):
                ring_copy(step, way, k).wait_send()
        return carry

    lax.fori_loop(1, half, drain, 0)


def body(theta, block_dims, pair_mask, term_charge, left_env, right_env, site_one, site_two):
    sectors, cap, pairs, _ = theta.shape
    terms = left_env.shape[0]
    half = lax.axis_size("mpo") // 2
    rc = cap // (2 * half)
    dims_v = jnp.broadcast_to(
        jnp.pad(block_dims.astype(F32), ((0, 0), (0, 6)))[:, :, None], (sectors, 8, cap)
    )
    anywhere = pl.BlockSpec(memory_space=pl.ANY)
    vmem = pl.BlockSpec(memory_space=pltpu.VMEM)
    smem = pl.BlockSpec(memory_space=pltpu.SMEM)
    return pl.pallas_call(
        kernel,
        out_shape=jax.ShapeDtypeStruct((sectors, rc, pairs, cap), F32),
        in_specs=[anywhere] * 3 + [vmem] + [smem] * 5,
        out_specs=vmem,
        scratch_shapes=[
            pltpu.VMEM((sectors, cap * pairs, cap), F32),
            pltpu.VMEM((2, cap * pairs, cap), F32),
            pltpu.VMEM(left_env.shape, F32),
            pltpu.VMEM(right_env.shape, F32),
            pltpu.VMEM((2, 8, cap), F32),
            pltpu.VMEM((4, 8, cap), F32),
            pltpu.VMEM((4, cap // CB, pairs * CB, 2 * cap), BF16),
            pltpu.VMEM((2 * terms, 2 * cap, pairs * cap), BF16),
            pltpu.VMEM((half, 2, terms, 4 * rc, 2 * cap), BF16),
            pltpu.VMEM((half, 2, 2, rc, pairs * cap), F32),
            pltpu.VMEM((half, 2, 2, rc, pairs * cap), F32),
            pltpu.SemaphoreType.DMA((3,)),
            pltpu.SemaphoreType.DMA((2, 2)),
            pltpu.SemaphoreType.DMA((2, 2)),
            pltpu.SemaphoreType.DMA((half, 2, 2)),
            pltpu.SemaphoreType.DMA((half, 2, 2)),
        ],
        compiler_params=pltpu.CompilerParams(
            collective_id=0, has_side_effects=True, vmem_limit_bytes=60 * 2**20
        ),
    )(
        theta.reshape(sectors, cap * pairs, cap), left_env, right_env, dims_v, block_dims, term_charge,
        pair_mask, site_one, site_two,
    )


def solution(mesh):
    placed = (
        P("blk", None, None, None),
        P("blk", None),
        P(None, "blk"),
        P(),
        P("mpo", "blk", None, None),
        P("mpo", "blk", None, None),
        P(),
        P(),
    )
    return jax.shard_map(
        body, mesh=mesh, in_specs=placed, out_specs=P("blk", "mpo", None, None), check_vma=False
    )
```

```python
import functools

import jax
import jax.numpy as jnp
from jax import lax
from jax.experimental import pallas as pl
from jax.experimental.pallas import tpu as pltpu
from jax.sharding import PartitionSpec as P

MESH = pl.DeviceIdType.MESH
F32 = jnp.float32
BF16 = jnp.bfloat16
CB = 32
RB = 16
WIDE = 1024


def halves(x):
    high = x.astype(BF16)
    return high, (x - high.astype(F32)).astype(BF16)


def kernel(
    theta, left, right, dims_s, charge, pair, one, two,
    out,
    theta_v, halo_v, left_v, right_v, dims_v, dims_halo, dims_all, split, weights, mixed, rows, part, arrived,
    local_sem, halo_send, halo_recv, ring_send, ring_recv,
):
    terms, _, cap, _ = left.shape
    site = one.shape[0]
    pairs = site * site
    n_blk, n = lax.axis_size("blk"), lax.axis_size("mpo")
    half = n // 2
    rc = cap // n
    blk, me = lax.axis_index("blk"), lax.axis_index("mpo")
    next_blk, last_blk = lax.rem(blk + 1, n_blk), lax.rem(blk + n_blk - 1, n_blk)
    up, down = lax.rem(me + 1, n), lax.rem(me + n - 1, n)
    w0 = me * terms

    local = [
        pltpu.make_async_copy(theta, theta_v, local_sem.at[0]),
        pltpu.make_async_copy(left, left_v, local_sem.at[1]),
        pltpu.make_async_copy(right, right_v, local_sem.at[2]),
    ]
    for copy in local:
        copy.start()

    for k in range(2):
        top = lax.broadcasted_iota(jnp.int32, (8, cap), 0) == 0
        dims_v[k] = jnp.where(top, dims_s[k, 0], dims_s[k, 1]).astype(F32)

    barrier = pltpu.get_barrier_semaphore()
    for target in ({"blk": next_blk}, {"blk": last_blk}, {"mpo": up}, {"mpo": down}):
        pl.semaphore_signal(barrier, inc=1, device_id=target, device_id_type=MESH)
    pl.semaphore_wait(barrier, 4)

    blocks = cap // CB
    span = CB * pairs

    def halo_copy(side, src, dst, sem):
        return pltpu.make_async_remote_copy(
            src_ref=src, dst_ref=dst, send_sem=halo_send.at[sem, side], recv_sem=halo_recv.at[sem, side],
            device_id={"blk": next_blk if side == 0 else last_blk}, device_id_type=MESH,
        )

    def halo_block(side, cb):
        start = pl.multiple_of(cb * span, span)
        return halo_copy(
            side, theta.at[1 - side, pl.ds(start, span)], halo_v.at[side, pl.ds(start, span)], cb
        )

    halo_dims = [halo_copy(side, dims_v.at[1 - side], dims_halo.at[side], blocks) for side in (0, 1)]
    for copy in halo_dims:
        copy.start()
    for cb in range(blocks):
        for side in (0, 1):
            halo_block(side, cb).start()

    def prepare(source, block_ref, index, cb):
        for q in range(pairs):
            high, low = halves(block_ref[index, pl.ds(cb * span + q, CB, stride=pairs), :])
            split[source, cb, pl.ds(q * CB, CB), pl.ds(0, cap)] = high
            split[source, cb, pl.ds(q * CB, CB), pl.ds(cap, cap)] = low

    lane = lax.broadcasted_iota(jnp.int32, (8, cap), 1).astype(F32)[0:1]

    def weigh(slot, w, k, source):
        row = dims_all[source]
        high, low = halves(jnp.where(lane < row[1:2], right_v[w, k], 0.0))
        weights[slot, pl.ds(0, cap), pl.ds(0, cap)] = high
        weights[slot, pl.ds(0, cap), pl.ds(cap, cap)] = high
        weights[slot, pl.ds(cap, cap), pl.ds(0, cap)] = low
        weights[slot, pl.ds(cap, cap), pl.ds(cap, cap)] = jnp.zeros_like(low)

    def apply_right(slot, w, k, source, cb):
        allowed = pair[k, w0 + w].astype(F32)
        first = [[one[s, t, w0 + w] * allowed for t in range(site)] for s in range(site)]
        second = [[two[u, v, w0 + w] for v in range(site)] for u in range(site)]
        both = lax.dot_general(
            split[source, cb], weights[slot], (((1,), (1,)), ((), ())), preferred_element_type=F32
        )
        for r in range(0, CB, RB):
            z = []
            for t in range(site):
                y = [both[q * CB + r:q * CB + r + RB] for q in range(t * site, (t + 1) * site)]
                y = [block[:, :cap] + block[:, cap:] for block in y]
                z.append([sum(second[u][v] * y[v] for v in range(site)) for u in range(site)])
            start = pl.multiple_of(cb * CB + r, RB)
            for s in range(site):
                for u in range(site):
                    p = s * site + u
                    high, low = halves(sum(first[s][t] * z[t][u] for t in range(site)))
                    mixed[slot, pl.ds(start, RB), pl.ds(p * cap, cap)] = high
                    mixed[slot, pl.ds(cap + start, RB), pl.ds(p * cap, cap)] = low

    def near(w):
        q = charge[w0 + w]
        k = jnp.where(q == 1, 1, 0)
        return w, w, k, k + 1 - q

    def far(w):
        q = charge[w0 + w]
        k = jnp.where(q == 1, 0, 1)
        return terms + w, w, k, k + 1 - q

    def each(count, task):
        lax.fori_loop(0, count, lambda index, carry: (task(index), carry)[1], 0)

    dims_all[1] = dims_v[0]
    dims_all[2] = dims_v[1]
    local[0].wait()
    each(blocks, lambda cb: [prepare(1 + k, theta_v, k, cb) for k in range(2)])
    local[2].wait()
    each(terms, lambda w: weigh(*near(w)))

    def near_term(w):
        each(blocks, lambda cb: apply_right(*near(w), cb))

    each(terms, near_term)

    for side, source in ((0, 0), (1, 3)):
        halo_dims[side].wait()
        outside = blk == (0 if side == 0 else n_blk - 1)
        dims_all[source] = dims_halo[side] * jnp.where(outside, 0.0, 1.0)
    each(terms, lambda w: weigh(*far(w)))

    local[1].wait()

    def rotate(g, carry):
        ahead = pl.multiple_of(lax.rem(me + half - g, n) * rc, rc)
        behind = pl.multiple_of(jnp.where(g == 0, me, lax.rem(me + n - half + g, n)) * rc, rc)
        for w in range(terms):
            q = charge[w0 + w]
            for k in range(2):
                row = dims_all[k + 1 - q]
                block = jnp.concatenate(
                    [left_v[w, k, pl.ds(ahead, rc), :], left_v[w, k, pl.ds(behind, rc), :]], axis=0
                )
                high, low = halves(jnp.where(lane < row[0:1], block, 0.0))
                rows[g, k, w] = jnp.concatenate(
                    [
                        jnp.concatenate([high, high], axis=1),
                        jnp.concatenate([low, jnp.zeros_like(low)], axis=1),
                    ],
                    axis=0,
                )
        return carry

    lax.fori_loop(0, half, rotate, 0)

    def far_block(cb):
        for side, source in ((0, 0), (1, 3)):
            halo_block(side, cb).wait_recv()
            prepare(source, halo_v, side, cb)
        each(terms, lambda w: apply_right(*far(w), cb))

    each(blocks, far_block)

    wide = WIDE
    pieces = pairs * cap // wide

    def columns(c):
        return pl.ds(pl.multiple_of(c * wide, wide), wide)

    def compute(g, k, c):
        total = jnp.zeros((4 * rc, wide), F32)
        for w in range(terms):
            q = charge[w0 + w]
            slot = w + jnp.where((q == 1) == (k == 1), 0, terms)
            total += jnp.dot(
                rows[g, k, w], mixed[slot, :, columns(c)], preferred_element_type=F32
            )
        total = total[:2 * rc] + total[2 * rc:]
        part[g, 0, k, :, columns(c)] = total[:rc]
        part[g, 1, k, :, columns(c)] = total[rc:]

    def ring_copy(step, way, k, c):
        row = 0 if isinstance(step, int) and step == 0 else way
        return pltpu.make_async_remote_copy(
            src_ref=part.at[step, row, k, :, columns(c)], dst_ref=arrived.at[step, way, k, :, columns(c)],
            send_sem=ring_send.at[step, way, k, c], recv_sem=ring_recv.at[step, way, k, c],
            device_id={"mpo": up if way == 0 else down}, device_id_type=MESH,
        )

    def forward(step, way, k, c):
        ring_copy(step - 1, way, k, c).wait_recv()
        part[step, way, k, :, columns(c)] += arrived[step - 1, way, k, :, columns(c)]
        ring_copy(step, way, k, c).start()

    for k in range(2):

        def farthest(c):
            compute(0, k, c)
            ring_copy(0, k, k, c).start()

        each(pieces, farthest)
    for k in range(2):

        def second(c):
            compute(1, k, c)
            ring_copy(1, 1 - k, k, c).start()
            forward(1, k, k, c)

        each(pieces, second)

    def later(step, carry):
        def piece(index):
            k, c = index // pieces, lax.rem(index, pieces)
            compute(step, k, c)
            for way in range(2):
                forward(step, way, k, c)

        each(2 * pieces, piece)
        return carry

    lax.fori_loop(2, half, later, 0)

    for k in range(2):
        row = lax.broadcasted_iota(jnp.int32, (rc, cap), 0) + me * rc
        column = lax.broadcasted_iota(jnp.int32, (rc, cap), 1)
        keep = (row < dims_s[k, 0]) & (column < dims_s[k, 1])
        for c in range(pieces):
            total = part[0, 1, k, :, c * wide:(c + 1) * wide]
            for way in range(2):
                ring_copy(half - 1, way, k, c).wait_recv()
                total = total + arrived[half - 1, way, k, :, c * wide:(c + 1) * wide]
            for p in range(wide // cap):
                out[k, :, c * (wide // cap) + p, :] = jnp.where(keep, total[:, p * cap:(p + 1) * cap], 0.0)

    def drain(c):
        for k in range(2):
            ring_copy(0, k, k, c).wait_send()
            for way in range(2):
                each(half - 1, lambda step: ring_copy(step + 1, way, k, c).wait_send())

    each(pieces, drain)
    each(blocks, lambda cb: [halo_block(side, cb).wait_send() for side in (0, 1)])


def body(theta, block_dims, pair_mask, term_charge, left_env, right_env, site_one, site_two):
    sectors, cap, pairs, _ = theta.shape
    terms = left_env.shape[0]
    half = lax.axis_size("mpo") // 2
    rc = cap // (2 * half)
    anywhere = pl.BlockSpec(memory_space=pl.ANY)
    vmem = pl.BlockSpec(memory_space=pltpu.VMEM)
    smem = pl.BlockSpec(memory_space=pltpu.SMEM)
    return pl.pallas_call(
        kernel,
        out_shape=jax.ShapeDtypeStruct((sectors, rc, pairs, cap), F32),
        in_specs=[anywhere] * 3 + [smem] * 5,
        out_specs=vmem,
        scratch_shapes=[
            pltpu.VMEM((sectors, cap * pairs, cap), F32),
            pltpu.VMEM((2, cap * pairs, cap), F32),
            pltpu.VMEM(left_env.shape, F32),
            pltpu.VMEM(right_env.shape, F32),
            pltpu.VMEM((2, 8, cap), F32),
            pltpu.VMEM((2, 8, cap), F32),
            pltpu.VMEM((4, 8, cap), F32),
            pltpu.VMEM((4, cap // CB, pairs * CB, 2 * cap), BF16),
            pltpu.VMEM((2 * terms, 2 * cap, 2 * cap), BF16),
            pltpu.VMEM((2 * terms, 2 * cap, pairs * cap), BF16),
            pltpu.VMEM((half, 2, terms, 4 * rc, 2 * cap), BF16),
            pltpu.VMEM((half, 2, 2, rc, pairs * cap), F32),
            pltpu.VMEM((half, 2, 2, rc, pairs * cap), F32),
            pltpu.SemaphoreType.DMA((3,)),
            pltpu.SemaphoreType.DMA((cap // CB + 1, 2)),
            pltpu.SemaphoreType.DMA((cap // CB + 1, 2)),
            pltpu.SemaphoreType.DMA((half, 2, 2, pairs * cap // WIDE)),
            pltpu.SemaphoreType.DMA((half, 2, 2, pairs * cap // WIDE)),
        ],
        compiler_params=pltpu.CompilerParams(
            collective_id=0, has_side_effects=True, vmem_limit_bytes=60 * 2**20
        ),
    )(
        theta.reshape(sectors, cap * pairs, cap), left_env, right_env, block_dims, term_charge,
        pair_mask.T, jnp.transpose(site_one, (1, 2, 0)), jnp.transpose(site_two, (1, 2, 0)),
    )


def solution(mesh):
    placed = (
        P("blk", None, None, None),
        P("blk", None),
        P(None, "blk"),
        P(),
        P("mpo", "blk", None, None),
        P("mpo", "blk", None, None),
        P(),
        P(),
    )
    return jax.shard_map(
        body, mesh=mesh, in_specs=placed, out_specs=P("blk", "mpo", None, None), check_vma=False
    )
```

```python
import functools

import jax
import jax.numpy as jnp
from jax import lax
from jax.experimental import pallas as pl
from jax.experimental.pallas import tpu as pltpu
from jax.sharding import PartitionSpec as P

MESH = pl.DeviceIdType.MESH
F32 = jnp.float32
BF16 = jnp.bfloat16
CB = 32
RB = 16
WIDE = 1024


def halves(x):
    high = x.astype(BF16)
    return high, (x - high.astype(F32)).astype(BF16)


def kernel(
    theta, left, right, dims_s, charge, pair, one, two,
    out,
    theta_v, halo_v, left_v, right_v, dims_v, dims_halo, dims_all, split, weights, mixed, rows, part, arrived,
    local_sem, halo_send, halo_recv, ring_send, ring_recv,
):
    terms, _, cap, _ = left.shape
    site = one.shape[0]
    pairs = site * site
    n_blk, n = lax.axis_size("blk"), lax.axis_size("mpo")
    half = n // 2
    rc = cap // n
    blk, me = lax.axis_index("blk"), lax.axis_index("mpo")
    next_blk, last_blk = lax.rem(blk + 1, n_blk), lax.rem(blk + n_blk - 1, n_blk)
    up, down = lax.rem(me + 1, n), lax.rem(me + n - 1, n)
    w0 = me * terms

    local = [
        pltpu.make_async_copy(theta, theta_v, local_sem.at[0]),
        pltpu.make_async_copy(left, left_v, local_sem.at[1]),
        pltpu.make_async_copy(right, right_v, local_sem.at[2]),
    ]
    for copy in local:
        copy.start()

    for k in range(2):
        top = lax.broadcasted_iota(jnp.int32, (8, cap), 0) == 0
        dims_v[k] = jnp.where(top, dims_s[k, 0], dims_s[k, 1]).astype(F32)

    barrier = pltpu.get_barrier_semaphore()
    for target in ({"blk": next_blk}, {"blk": last_blk}, {"mpo": up}, {"mpo": down}):
        pl.semaphore_signal(barrier, inc=1, device_id=target, device_id_type=MESH)
    pl.semaphore_wait(barrier, 4)

    blocks = cap // CB
    span = CB * pairs

    def halo_copy(side, src, dst, sem):
        return pltpu.make_async_remote_copy(
            src_ref=src, dst_ref=dst, send_sem=halo_send.at[sem, side], recv_sem=halo_recv.at[sem, side],
            device_id={"blk": next_blk if side == 0 else last_blk}, device_id_type=MESH,
        )

    def halo_block(side, cb):
        start = pl.multiple_of(cb * span, span)
        return halo_copy(
            side, theta.at[1 - side, pl.ds(start, span)], halo_v.at[side, pl.ds(start, span)], cb
        )

    halo_dims = [halo_copy(side, dims_v.at[1 - side], dims_halo.at[side], blocks) for side in (0, 1)]
    for copy in halo_dims:
        copy.start()
    for cb in range(blocks):
        for side in (0, 1):
            halo_block(side, cb).start()

    def prepare(source, block_ref, index, cb):
        for q in range(pairs):
            high, low = halves(block_ref[index, pl.ds(cb * span + q, CB, stride=pairs), :])
            split[source, cb, pl.ds(q * CB, CB), pl.ds(0, cap)] = high
            split[source, cb, pl.ds(q * CB, CB), pl.ds(cap, cap)] = low

    lane = lax.broadcasted_iota(jnp.int32, (8, cap), 1).astype(F32)[0:1]

    def weigh(slot, w, k, source):
        row = dims_all[source]
        high, low = halves(jnp.where(lane < row[1:2], right_v[w, k], 0.0))
        weights[slot, pl.ds(0, cap), pl.ds(0, cap)] = high
        weights[slot, pl.ds(0, cap), pl.ds(cap, cap)] = high
        weights[slot, pl.ds(cap, cap), pl.ds(0, cap)] = low
        weights[slot, pl.ds(cap, cap), pl.ds(cap, cap)] = jnp.zeros_like(low)

    def apply_right(slot, w, k, source, cb):
        allowed = pair[k, w0 + w].astype(F32)
        first = [[one[s, t, w0 + w] * allowed for t in range(site)] for s in range(site)]
        second = [[two[u, v, w0 + w] for v in range(site)] for u in range(site)]
        both = lax.dot_general(
            split[source, cb], weights[slot], (((1,), (1,)), ((), ())), preferred_element_type=F32
        )
        for r in range(0, CB, RB):
            z = []
            for t in range(site):
                y = [both[q * CB + r:q * CB + r + RB] for q in range(t * site, (t + 1) * site)]
                y = [block[:, :cap] + block[:, cap:] for block in y]
                z.append([sum(second[u][v] * y[v] for v in range(site)) for u in range(site)])
            start = pl.multiple_of(cb * CB + r, RB)
            for s in range(site):
                for u in range(site):
                    p = s * site + u
                    high, low = halves(sum(first[s][t] * z[t][u] for t in range(site)))
                    mixed[slot, pl.ds(start, RB), pl.ds(p * cap, cap)] = high
                    mixed[slot, pl.ds(cap + start, RB), pl.ds(p * cap, cap)] = low

    def near(w):
        q = charge[w0 + w]
        k = jnp.where(q == 1, 1, 0)
        return w, w, k, k + 1 - q

    def far(w):
        q = charge[w0 + w]
        k = jnp.where(q == 1, 0, 1)
        return terms + w, w, k, k + 1 - q

    def each(count, task, unroll=1):
        lax.fori_loop(0, count, lambda index, carry: (task(index), carry)[1], 0, unroll=unroll)

    dims_all[1] = dims_v[0]
    dims_all[2] = dims_v[1]
    local[0].wait()
    each(blocks, lambda cb: [prepare(1 + k, theta_v, k, cb) for k in range(2)])
    local[2].wait()
    each(terms, lambda w: weigh(*near(w)))

    def near_term(w):
        each(blocks, lambda cb: apply_right(*near(w), cb), 4)

    each(terms, near_term)

    for side, source in ((0, 0), (1, 3)):
        halo_dims[side].wait()
        outside = blk == (0 if side == 0 else n_blk - 1)
        dims_all[source] = dims_halo[side] * jnp.where(outside, 0.0, 1.0)
    each(terms, lambda w: weigh(*far(w)))

    local[1].wait()

    def rotate(g):
        ahead = pl.multiple_of(lax.rem(me + half - g, n) * rc, rc)
        behind = pl.multiple_of(jnp.where(g == 0, me, lax.rem(me + n - half + g, n)) * rc, rc)
        for w in range(terms):
            q = charge[w0 + w]
            for k in range(2):
                row = dims_all[k + 1 - q]
                block = jnp.concatenate(
                    [left_v[w, k, pl.ds(ahead, rc), :], left_v[w, k, pl.ds(behind, rc), :]], axis=0
                )
                high, low = halves(jnp.where(lane < row[0:1], block, 0.0))
                rows[g, k, w] = jnp.concatenate(
                    [
                        jnp.concatenate([high, high], axis=1),
                        jnp.concatenate([low, jnp.zeros_like(low)], axis=1),
                    ],
                    axis=0,
                )

    def far_block(cb):
        for side, source in ((0, 0), (1, 3)):
            halo_block(side, cb).wait_recv()
            prepare(source, halo_v, side, cb)
        each(terms, lambda w: apply_right(*far(w), cb), 3)

    each(blocks, far_block)

    wide = WIDE
    pieces = pairs * cap // wide

    def columns(c):
        return pl.ds(pl.multiple_of(c * wide, wide), wide)

    def compute(g, k, c):
        total = jnp.zeros((4 * rc, wide), F32)
        for w in range(terms):
            q = charge[w0 + w]
            slot = w + jnp.where((q == 1) == (k == 1), 0, terms)
            total += jnp.dot(
                rows[g, k, w], mixed[slot, :, columns(c)], preferred_element_type=F32
            )
        total = total[:2 * rc] + total[2 * rc:]
        part[g, 0, k, :, columns(c)] = total[:rc]
        part[g, 1, k, :, columns(c)] = total[rc:]

    def ring_copy(step, way, k, c):
        row = 0 if isinstance(step, int) and step == 0 else way
        return pltpu.make_async_remote_copy(
            src_ref=part.at[step, row, k, :, columns(c)], dst_ref=arrived.at[step, way, k, :, columns(c)],
            send_sem=ring_send.at[step, way, k, c], recv_sem=ring_recv.at[step, way, k, c],
            device_id={"mpo": up if way == 0 else down}, device_id_type=MESH,
        )

    def forward(step, way, k, c):
        ring_copy(step - 1, way, k, c).wait_recv()
        part[step, way, k, :, columns(c)] += arrived[step - 1, way, k, :, columns(c)]
        ring_copy(step, way, k, c).start()

    rotate(0)
    for k in range(2):

        def farthest(c):
            compute(0, k, c)
            ring_copy(0, k, k, c).start()

        each(pieces, farthest)
    rotate(1)
    for k in range(2):

        def second(c):
            compute(1, k, c)
            ring_copy(1, 1 - k, k, c).start()
            forward(1, k, k, c)

        each(pieces, second)

    def later(step, carry):
        rotate(step)

        def piece(index):
            k, c = index // pieces, lax.rem(index, pieces)
            compute(step, k, c)
            for way in range(2):
                forward(step, way, k, c)

        each(2 * pieces, piece)
        return carry

    lax.fori_loop(2, half, later, 0)

    for k in range(2):
        row = lax.broadcasted_iota(jnp.int32, (rc, cap), 0) + me * rc
        column = lax.broadcasted_iota(jnp.int32, (rc, cap), 1)
        keep = (row < dims_s[k, 0]) & (column < dims_s[k, 1])
        for c in range(pieces):
            total = part[0, 1, k, :, c * wide:(c + 1) * wide]
            for way in range(2):
                ring_copy(half - 1, way, k, c).wait_recv()
                total = total + arrived[half - 1, way, k, :, c * wide:(c + 1) * wide]
            for p in range(wide // cap):
                out[k, :, c * (wide // cap) + p, :] = jnp.where(keep, total[:, p * cap:(p + 1) * cap], 0.0)

    def drain(c):
        for k in range(2):
            ring_copy(0, k, k, c).wait_send()
            for way in range(2):
                each(half - 1, lambda step: ring_copy(step + 1, way, k, c).wait_send())

    each(pieces, drain)
    each(blocks, lambda cb: [halo_block(side, cb).wait_send() for side in (0, 1)])


def body(theta, block_dims, pair_mask, term_charge, left_env, right_env, site_one, site_two):
    sectors, cap, pairs, _ = theta.shape
    terms = left_env.shape[0]
    half = lax.axis_size("mpo") // 2
    rc = cap // (2 * half)
    anywhere = pl.BlockSpec(memory_space=pl.ANY)
    vmem = pl.BlockSpec(memory_space=pltpu.VMEM)
    smem = pl.BlockSpec(memory_space=pltpu.SMEM)
    return pl.pallas_call(
        kernel,
        out_shape=jax.ShapeDtypeStruct((sectors, rc, pairs, cap), F32),
        in_specs=[anywhere] * 3 + [smem] * 5,
        out_specs=vmem,
        scratch_shapes=[
            pltpu.VMEM((sectors, cap * pairs, cap), F32),
            pltpu.VMEM((2, cap * pairs, cap), F32),
            pltpu.VMEM(left_env.shape, F32),
            pltpu.VMEM(right_env.shape, F32),
            pltpu.VMEM((2, 8, cap), F32),
            pltpu.VMEM((2, 8, cap), F32),
            pltpu.VMEM((4, 8, cap), F32),
            pltpu.VMEM((4, cap // CB, pairs * CB, 2 * cap), BF16),
            pltpu.VMEM((2 * terms, 2 * cap, 2 * cap), BF16),
            pltpu.VMEM((2 * terms, 2 * cap, pairs * cap), BF16),
            pltpu.VMEM((half, 2, terms, 4 * rc, 2 * cap), BF16),
            pltpu.VMEM((half, 2, 2, rc, pairs * cap), F32),
            pltpu.VMEM((half, 2, 2, rc, pairs * cap), F32),
            pltpu.SemaphoreType.DMA((3,)),
            pltpu.SemaphoreType.DMA((cap // CB + 1, 2)),
            pltpu.SemaphoreType.DMA((cap // CB + 1, 2)),
            pltpu.SemaphoreType.DMA((half, 2, 2, pairs * cap // WIDE)),
            pltpu.SemaphoreType.DMA((half, 2, 2, pairs * cap // WIDE)),
        ],
        compiler_params=pltpu.CompilerParams(
            collective_id=0, has_side_effects=True, vmem_limit_bytes=60 * 2**20
        ),
    )(
        theta.reshape(sectors, cap * pairs, cap), left_env, right_env, block_dims, term_charge,
        pair_mask.T, jnp.transpose(site_one, (1, 2, 0)), jnp.transpose(site_two, (1, 2, 0)),
    )


def solution(mesh):
    placed = (
        P("blk", None, None, None),
        P("blk", None),
        P(None, "blk"),
        P(),
        P("mpo", "blk", None, None),
        P("mpo", "blk", None, None),
        P(),
        P(),
    )
    return jax.shard_map(
        body, mesh=mesh, in_specs=placed, out_specs=P("blk", "mpo", None, None), check_vma=False
    )
```

```python
import functools

import jax
import jax.numpy as jnp
from jax import lax
from jax.experimental import pallas as pl
from jax.experimental.pallas import tpu as pltpu
from jax.sharding import PartitionSpec as P

MESH = pl.DeviceIdType.MESH
F32 = jnp.float32
BF16 = jnp.bfloat16
CB = 16
RB = 16
WIDE = 1024


def halves(x):
    high = x.astype(BF16)
    return high, (x - high.astype(F32)).astype(BF16)


def kernel(
    theta, left, right, dims_s, charge, pair, one, two,
    out,
    theta_v, halo_v, left_v, right_v, dims_v, dims_halo, dims_all, split, weights, mixed, rows, part, arrived,
    local_sem, halo_send, halo_recv, ring_send, ring_recv,
):
    terms, _, cap, _ = left.shape
    site = one.shape[0]
    pairs = site * site
    n_blk, n = lax.axis_size("blk"), lax.axis_size("mpo")
    half = n // 2
    rc = cap // n
    blk, me = lax.axis_index("blk"), lax.axis_index("mpo")
    next_blk, last_blk = lax.rem(blk + 1, n_blk), lax.rem(blk + n_blk - 1, n_blk)
    up, down = lax.rem(me + 1, n), lax.rem(me + n - 1, n)
    w0 = me * terms

    local = [
        pltpu.make_async_copy(theta, theta_v, local_sem.at[0]),
        pltpu.make_async_copy(left, left_v, local_sem.at[1]),
        pltpu.make_async_copy(right, right_v, local_sem.at[2]),
    ]
    for copy in local:
        copy.start()

    for k in range(2):
        top = lax.broadcasted_iota(jnp.int32, (8, cap), 0) == 0
        dims_v[k] = jnp.where(top, dims_s[k, 0], dims_s[k, 1]).astype(F32)

    barrier = pltpu.get_barrier_semaphore()
    for target in ({"blk": next_blk}, {"blk": last_blk}, {"mpo": up}, {"mpo": down}):
        pl.semaphore_signal(barrier, inc=1, device_id=target, device_id_type=MESH)
    pl.semaphore_wait(barrier, 4)

    blocks = cap // CB
    span = CB * pairs

    def halo_copy(side, src, dst, sem):
        return pltpu.make_async_remote_copy(
            src_ref=src, dst_ref=dst, send_sem=halo_send.at[sem, side], recv_sem=halo_recv.at[sem, side],
            device_id={"blk": next_blk if side == 0 else last_blk}, device_id_type=MESH,
        )

    def halo_block(side, cb):
        start = pl.multiple_of(cb * span, span)
        return halo_copy(
            side, theta.at[1 - side, pl.ds(start, span)], halo_v.at[side, pl.ds(start, span)], cb
        )

    halo_dims = [halo_copy(side, dims_v.at[1 - side], dims_halo.at[side], blocks) for side in (0, 1)]
    for copy in halo_dims:
        copy.start()
    for cb in range(blocks):
        for side in (0, 1):
            halo_block(side, cb).start()

    def prepare(source, block_ref, index, cb):
        for q in range(pairs):
            high, low = halves(block_ref[index, pl.ds(cb * span + q, CB, stride=pairs), :])
            split[source, cb, pl.ds(q * CB, CB), pl.ds(0, cap)] = high
            split[source, cb, pl.ds(q * CB, CB), pl.ds(cap, cap)] = low

    lane = lax.broadcasted_iota(jnp.int32, (8, cap), 1).astype(F32)[0:1]

    def weigh(slot, w, k, source):
        row = dims_all[source]
        high, low = halves(jnp.where(lane < row[1:2], right_v[w, k], 0.0))
        weights[slot, pl.ds(0, cap), pl.ds(0, cap)] = high
        weights[slot, pl.ds(0, cap), pl.ds(cap, cap)] = high
        weights[slot, pl.ds(cap, cap), pl.ds(0, cap)] = low
        weights[slot, pl.ds(cap, cap), pl.ds(cap, cap)] = jnp.zeros_like(low)

    def apply_right(slot, w, k, source, cb):
        allowed = pair[k, w0 + w].astype(F32)
        first = [[one[s, t, w0 + w] * allowed for t in range(site)] for s in range(site)]
        second = [[two[u, v, w0 + w] for v in range(site)] for u in range(site)]
        both = lax.dot_general(
            split[source, cb], weights[slot], (((1,), (1,)), ((), ())), preferred_element_type=F32
        )
        for r in range(0, CB, RB):
            z = []
            for t in range(site):
                y = [both[q * CB + r:q * CB + r + RB] for q in range(t * site, (t + 1) * site)]
                y = [block[:, :cap] + block[:, cap:] for block in y]
                z.append([sum(second[u][v] * y[v] for v in range(site)) for u in range(site)])
            start = pl.multiple_of(cb * CB + r, RB)
            for s in range(site):
                for u in range(site):
                    p = s * site + u
                    high, low = halves(sum(first[s][t] * z[t][u] for t in range(site)))
                    mixed[slot, pl.ds(start, RB), pl.ds(p * cap, cap)] = high
                    mixed[slot, pl.ds(cap + start, RB), pl.ds(p * cap, cap)] = low

    def near(w):
        q = charge[w0 + w]
        k = jnp.where(q == 1, 1, 0)
        return w, w, k, k + 1 - q

    def far(w):
        q = charge[w0 + w]
        k = jnp.where(q == 1, 0, 1)
        return terms + w, w, k, k + 1 - q

    def each(count, task, unroll=1):
        lax.fori_loop(0, count, lambda index, carry: (task(index), carry)[1], 0, unroll=unroll)

    dims_all[1] = dims_v[0]
    dims_all[2] = dims_v[1]
    local[0].wait()
    each(blocks, lambda cb: [prepare(1 + k, theta_v, k, cb) for k in range(2)])
    local[2].wait()
    each(terms, lambda w: weigh(*near(w)))

    def near_term(w):
        each(blocks, lambda cb: apply_right(*near(w), cb), 8)

    each(terms, near_term)

    for side, source in ((0, 0), (1, 3)):
        halo_dims[side].wait()
        outside = blk == (0 if side == 0 else n_blk - 1)
        dims_all[source] = dims_halo[side] * jnp.where(outside, 0.0, 1.0)
    each(terms, lambda w: weigh(*far(w)))

    local[1].wait()

    def rotate(g):
        ahead = pl.multiple_of(lax.rem(me + half - g, n) * rc, rc)
        behind = pl.multiple_of(jnp.where(g == 0, me, lax.rem(me + n - half + g, n)) * rc, rc)
        for w in range(terms):
            q = charge[w0 + w]
            for k in range(2):
                row = dims_all[k + 1 - q]
                block = jnp.concatenate(
                    [left_v[w, k, pl.ds(ahead, rc), :], left_v[w, k, pl.ds(behind, rc), :]], axis=0
                )
                high, low = halves(jnp.where(lane < row[0:1], block, 0.0))
                rows[g, k, w] = jnp.concatenate(
                    [
                        jnp.concatenate([high, high], axis=1),
                        jnp.concatenate([low, jnp.zeros_like(low)], axis=1),
                    ],
                    axis=0,
                )

    def far_block(cb):
        for side, source in ((0, 0), (1, 3)):
            halo_block(side, cb).wait_recv()
            prepare(source, halo_v, side, cb)
        each(terms, lambda w: apply_right(*far(w), cb), 6)

    each(blocks, far_block)

    wide = WIDE
    pieces = pairs * cap // wide

    def columns(c):
        return pl.ds(pl.multiple_of(c * wide, wide), wide)

    def compute(g, k, c):
        total = jnp.zeros((4 * rc, wide), F32)
        for w in range(terms):
            q = charge[w0 + w]
            slot = w + jnp.where((q == 1) == (k == 1), 0, terms)
            total += jnp.dot(
                rows[g, k, w], mixed[slot, :, columns(c)], preferred_element_type=F32
            )
        total = total[:2 * rc] + total[2 * rc:]
        part[g, 0, k, :, columns(c)] = total[:rc]
        part[g, 1, k, :, columns(c)] = total[rc:]

    def ring_copy(step, way, k, c):
        row = 0 if isinstance(step, int) and step == 0 else way
        return pltpu.make_async_remote_copy(
            src_ref=part.at[step, row, k, :, columns(c)], dst_ref=arrived.at[step, way, k, :, columns(c)],
            send_sem=ring_send.at[step, way, k, c], recv_sem=ring_recv.at[step, way, k, c],
            device_id={"mpo": up if way == 0 else down}, device_id_type=MESH,
        )

    def forward(step, way, k, c):
        ring_copy(step - 1, way, k, c).wait_recv()
        part[step, way, k, :, columns(c)] += arrived[step - 1, way, k, :, columns(c)]
        ring_copy(step, way, k, c).start()

    rotate(0)
    for k in range(2):

        def farthest(c):
            compute(0, k, c)
            ring_copy(0, k, k, c).start()

        each(pieces, farthest)
    rotate(1)
    for k in range(2):

        def second(c):
            compute(1, k, c)
            ring_copy(1, 1 - k, k, c).start()
            forward(1, k, k, c)

        each(pieces, second)

    def later(step, carry):
        rotate(step)

        def piece(index):
            k, c = index // pieces, lax.rem(index, pieces)
            compute(step, k, c)
            for way in range(2):
                forward(step, way, k, c)

        each(2 * pieces, piece)
        return carry

    lax.fori_loop(2, half, later, 0)

    for k in range(2):
        row = lax.broadcasted_iota(jnp.int32, (rc, cap), 0) + me * rc
        column = lax.broadcasted_iota(jnp.int32, (rc, cap), 1)
        keep = (row < dims_s[k, 0]) & (column < dims_s[k, 1])
        for c in range(pieces):
            total = part[0, 1, k, :, c * wide:(c + 1) * wide]
            for way in range(2):
                ring_copy(half - 1, way, k, c).wait_recv()
                total = total + arrived[half - 1, way, k, :, c * wide:(c + 1) * wide]
            for p in range(wide // cap):
                out[k, :, c * (wide // cap) + p, :] = jnp.where(keep, total[:, p * cap:(p + 1) * cap], 0.0)

    def drain(c):
        for k in range(2):
            ring_copy(0, k, k, c).wait_send()
            for way in range(2):
                each(half - 1, lambda step: ring_copy(step + 1, way, k, c).wait_send())

    each(pieces, drain)
    each(blocks, lambda cb: [halo_block(side, cb).wait_send() for side in (0, 1)])


def body(theta, block_dims, pair_mask, term_charge, left_env, right_env, site_one, site_two):
    sectors, cap, pairs, _ = theta.shape
    terms = left_env.shape[0]
    half = lax.axis_size("mpo") // 2
    rc = cap // (2 * half)
    anywhere = pl.BlockSpec(memory_space=pl.ANY)
    vmem = pl.BlockSpec(memory_space=pltpu.VMEM)
    smem = pl.BlockSpec(memory_space=pltpu.SMEM)
    return pl.pallas_call(
        kernel,
        out_shape=jax.ShapeDtypeStruct((sectors, rc, pairs, cap), F32),
        in_specs=[anywhere] * 3 + [smem] * 5,
        out_specs=vmem,
        scratch_shapes=[
            pltpu.VMEM((sectors, cap * pairs, cap), F32),
            pltpu.VMEM((2, cap * pairs, cap), F32),
            pltpu.VMEM(left_env.shape, F32),
            pltpu.VMEM(right_env.shape, F32),
            pltpu.VMEM((2, 8, cap), F32),
            pltpu.VMEM((2, 8, cap), F32),
            pltpu.VMEM((4, 8, cap), F32),
            pltpu.VMEM((4, cap // CB, pairs * CB, 2 * cap), BF16),
            pltpu.VMEM((2 * terms, 2 * cap, 2 * cap), BF16),
            pltpu.VMEM((2 * terms, 2 * cap, pairs * cap), BF16),
            pltpu.VMEM((half, 2, terms, 4 * rc, 2 * cap), BF16),
            pltpu.VMEM((half, 2, 2, rc, pairs * cap), F32),
            pltpu.VMEM((half, 2, 2, rc, pairs * cap), F32),
            pltpu.SemaphoreType.DMA((3,)),
            pltpu.SemaphoreType.DMA((cap // CB + 1, 2)),
            pltpu.SemaphoreType.DMA((cap // CB + 1, 2)),
            pltpu.SemaphoreType.DMA((half, 2, 2, pairs * cap // WIDE)),
            pltpu.SemaphoreType.DMA((half, 2, 2, pairs * cap // WIDE)),
        ],
        compiler_params=pltpu.CompilerParams(
            collective_id=0, has_side_effects=True, vmem_limit_bytes=60 * 2**20
        ),
    )(
        theta.reshape(sectors, cap * pairs, cap), left_env, right_env, block_dims, term_charge,
        pair_mask.T, jnp.transpose(site_one, (1, 2, 0)), jnp.transpose(site_two, (1, 2, 0)),
    )


def solution(mesh):
    placed = (
        P("blk", None, None, None),
        P("blk", None),
        P(None, "blk"),
        P(),
        P("mpo", "blk", None, None),
        P("mpo", "blk", None, None),
        P(),
        P(),
    )
    return jax.shard_map(
        body, mesh=mesh, in_specs=placed, out_specs=P("blk", "mpo", None, None), check_vma=False
    )
```

```python
import functools

import jax
import jax.numpy as jnp
from jax import lax
from jax.experimental import pallas as pl
from jax.experimental.pallas import tpu as pltpu
from jax.sharding import PartitionSpec as P

MESH = pl.DeviceIdType.MESH
F32 = jnp.float32
BF16 = jnp.bfloat16
CB = 16
RB = 16
WIDE = 1024


def halves(x):
    high = x.astype(BF16)
    return high, (x - high.astype(F32)).astype(BF16)


def kernel(
    theta, left, right, dims_s, charge, pair, one, two,
    out,
    theta_v, halo_v, left_v, right_v, dims_v, dims_halo, dims_all, split, weights, mixed, rows, part, arrived,
    local_sem, halo_send, halo_recv, ring_send, ring_recv,
):
    terms, _, cap, _ = left.shape
    site = one.shape[0]
    pairs = site * site
    n_blk, n = lax.axis_size("blk"), lax.axis_size("mpo")
    half = n // 2
    rc = cap // n
    blk, me = lax.axis_index("blk"), lax.axis_index("mpo")
    next_blk, last_blk = lax.rem(blk + 1, n_blk), lax.rem(blk + n_blk - 1, n_blk)
    up, down = lax.rem(me + 1, n), lax.rem(me + n - 1, n)
    w0 = me * terms

    local = [
        pltpu.make_async_copy(theta, theta_v, local_sem.at[0]),
        pltpu.make_async_copy(left, left_v, local_sem.at[1]),
        pltpu.make_async_copy(right, right_v, local_sem.at[2]),
    ]
    for copy in local:
        copy.start()

    for k in range(2):
        top = lax.broadcasted_iota(jnp.int32, (8, cap), 0) == 0
        dims_v[k] = jnp.where(top, dims_s[k, 0], dims_s[k, 1]).astype(F32)

    barrier = pltpu.get_barrier_semaphore()
    for target in ({"blk": next_blk}, {"blk": last_blk}, {"mpo": up}, {"mpo": down}):
        pl.semaphore_signal(barrier, inc=1, device_id=target, device_id_type=MESH)
    pl.semaphore_wait(barrier, 4)

    blocks = cap // CB
    span = CB * pairs

    def halo_copy(side, src, dst, sem):
        return pltpu.make_async_remote_copy(
            src_ref=src, dst_ref=dst, send_sem=halo_send.at[sem, side], recv_sem=halo_recv.at[sem, side],
            device_id={"blk": next_blk if side == 0 else last_blk}, device_id_type=MESH,
        )

    def halo_block(side, cb):
        start = pl.multiple_of(cb * span, span)
        return halo_copy(
            side, theta.at[1 - side, pl.ds(start, span)], halo_v.at[side, pl.ds(start, span)], cb
        )

    halo_dims = [halo_copy(side, dims_v.at[1 - side], dims_halo.at[side], blocks) for side in (0, 1)]
    for copy in halo_dims:
        copy.start()
    for cb in range(blocks):
        for side in (0, 1):
            halo_block(side, cb).start()

    def prepare(source, block_ref, index, cb):
        for q in range(pairs):
            high, low = halves(block_ref[index, pl.ds(cb * span + q, CB, stride=pairs), :])
            split[source, cb, pl.ds(q * CB, CB), pl.ds(0, cap)] = high
            split[source, cb, pl.ds(q * CB, CB), pl.ds(cap, cap)] = low

    lane = lax.broadcasted_iota(jnp.int32, (8, cap), 1).astype(F32)[0:1]

    def weigh(slot, w, k, source):
        row = dims_all[source]
        high, low = halves(jnp.where(lane < row[1:2], right_v[w, k], 0.0))
        weights[slot, pl.ds(0, cap), pl.ds(0, cap)] = high
        weights[slot, pl.ds(0, cap), pl.ds(cap, cap)] = high
        weights[slot, pl.ds(cap, cap), pl.ds(0, cap)] = low
        weights[slot, pl.ds(cap, cap), pl.ds(cap, cap)] = jnp.zeros_like(low)

    def apply_right(slot, w, k, source, cb):
        allowed = pair[k, w0 + w].astype(F32)
        first = [[one[s, t, w0 + w] * allowed for t in range(site)] for s in range(site)]
        second = [[two[u, v, w0 + w] for v in range(site)] for u in range(site)]
        both = lax.dot_general(
            split[source, cb], weights[slot], (((1,), (1,)), ((), ())), preferred_element_type=F32
        )
        for r in range(0, CB, RB):
            z = []
            for t in range(site):
                y = [both[q * CB + r:q * CB + r + RB] for q in range(t * site, (t + 1) * site)]
                y = [block[:, :cap] + block[:, cap:] for block in y]
                z.append([sum(second[u][v] * y[v] for v in range(site)) for u in range(site)])
            start = pl.multiple_of(cb * CB + r, RB)
            for s in range(site):
                for u in range(site):
                    p = s * site + u
                    high, low = halves(sum(first[s][t] * z[t][u] for t in range(site)))
                    mixed[slot, pl.ds(start, RB), pl.ds(p * cap, cap)] = high
                    mixed[slot, pl.ds(cap + start, RB), pl.ds(p * cap, cap)] = low

    def near(w):
        q = charge[w0 + w]
        k = jnp.where(q == 1, 1, 0)
        return w, w, k, k + 1 - q

    def far(w):
        q = charge[w0 + w]
        k = jnp.where(q == 1, 0, 1)
        return terms + w, w, k, k + 1 - q

    def each(count, task, unroll=1):
        lax.fori_loop(0, count, lambda index, carry: (task(index), carry)[1], 0, unroll=unroll)

    dims_all[1] = dims_v[0]
    dims_all[2] = dims_v[1]
    local[0].wait()
    each(blocks, lambda cb: [prepare(1 + k, theta_v, k, cb) for k in range(2)])
    local[2].wait()
    each(terms, lambda w: weigh(*near(w)))

    def near_term(w):
        each(blocks, lambda cb: apply_right(*near(w), cb), 8)

    each(terms, near_term)

    for side, source in ((0, 0), (1, 3)):
        halo_dims[side].wait()
        outside = blk == (0 if side == 0 else n_blk - 1)
        dims_all[source] = dims_halo[side] * jnp.where(outside, 0.0, 1.0)
    each(terms, lambda w: weigh(*far(w)))

    local[1].wait()

    def rotate(g):
        ahead = pl.multiple_of(lax.rem(me + half - g, n) * rc, rc)
        behind = pl.multiple_of(jnp.where(g == 0, me, lax.rem(me + n - half + g, n)) * rc, rc)
        for w in range(terms):
            q = charge[w0 + w]
            for k in range(2):
                row = dims_all[k + 1 - q]
                block = jnp.concatenate(
                    [left_v[w, k, pl.ds(ahead, rc), :], left_v[w, k, pl.ds(behind, rc), :]], axis=0
                )
                high, low = halves(jnp.where(lane < row[0:1], block, 0.0))
                rows[g, k, w] = jnp.concatenate(
                    [
                        jnp.concatenate([high, high], axis=1),
                        jnp.concatenate([low, jnp.zeros_like(low)], axis=1),
                    ],
                    axis=0,
                )

    def far_block(cb):
        for side, source in ((0, 0), (1, 3)):
            halo_block(side, cb).wait_recv()
            prepare(source, halo_v, side, cb)
        each(terms, lambda w: apply_right(*far(w), cb), 6)

    each(blocks, far_block)

    wide = WIDE
    pieces = pairs * cap // wide

    def columns(c):
        return pl.ds(pl.multiple_of(c * wide, wide), wide)

    def compute(g, k, c):
        total = jnp.zeros((4 * rc, wide), F32)
        for w in range(terms):
            q = charge[w0 + w]
            slot = w + jnp.where((q == 1) == (k == 1), 0, terms)
            total += jnp.dot(
                rows[g, k, w], mixed[slot, :, columns(c)], preferred_element_type=F32
            )
        total = total[:2 * rc] + total[2 * rc:]
        part[g, 0, k, :, columns(c)] = total[:rc]
        part[g, 1, k, :, columns(c)] = total[rc:]

    def compute_two(g, k, c):
        total = jnp.zeros((8 * rc, wide), F32)
        for w in range(terms):
            q = charge[w0 + w]
            slot = w + jnp.where((q == 1) == (k == 1), 0, terms)
            both = jnp.concatenate([rows[g, k, w], rows[g + 1, k, w]], axis=0)
            total += jnp.dot(both, mixed[slot, :, columns(c)], preferred_element_type=F32)
        for step in range(2):
            mine = total[step * 4 * rc:(step + 1) * 4 * rc]
            mine = mine[:2 * rc] + mine[2 * rc:]
            part[g + step, 0, k, :, columns(c)] = mine[:rc]
            part[g + step, 1, k, :, columns(c)] = mine[rc:]

    def ring_copy(step, way, k, c):
        row = 0 if isinstance(step, int) and step == 0 else way
        return pltpu.make_async_remote_copy(
            src_ref=part.at[step, row, k, :, columns(c)], dst_ref=arrived.at[step, way, k, :, columns(c)],
            send_sem=ring_send.at[step, way, k, c], recv_sem=ring_recv.at[step, way, k, c],
            device_id={"mpo": up if way == 0 else down}, device_id_type=MESH,
        )

    def forward(step, way, k, c):
        ring_copy(step - 1, way, k, c).wait_recv()
        part[step, way, k, :, columns(c)] += arrived[step - 1, way, k, :, columns(c)]
        ring_copy(step, way, k, c).start()

    rotate(0)
    for k in range(2):

        def farthest(c):
            compute(0, k, c)
            ring_copy(0, k, k, c).start()

        each(pieces, farthest)
    rotate(1)
    for k in range(2):

        def second(c):
            compute(1, k, c)
            ring_copy(1, 1 - k, k, c).start()
            forward(1, k, k, c)

        each(pieces, second)

    def later(index, carry):
        step = 2 * index
        rotate(step)
        rotate(step + 1)

        def piece(index):
            k, c = index // pieces, lax.rem(index, pieces)
            compute_two(step, k, c)
            for way in range(2):
                forward(step, way, k, c)

        def passed(index):
            for way in range(2):
                forward(step + 1, way, index // pieces, lax.rem(index, pieces))

        each(2 * pieces, piece)
        each(2 * pieces, passed)
        return carry

    assert half % 2 == 0
    lax.fori_loop(1, half // 2, later, 0)

    for k in range(2):
        row = lax.broadcasted_iota(jnp.int32, (rc, cap), 0) + me * rc
        column = lax.broadcasted_iota(jnp.int32, (rc, cap), 1)
        keep = (row < dims_s[k, 0]) & (column < dims_s[k, 1])
        for c in range(pieces):
            total = part[0, 1, k, :, c * wide:(c + 1) * wide]
            for way in range(2):
                ring_copy(half - 1, way, k, c).wait_recv()
                total = total + arrived[half - 1, way, k, :, c * wide:(c + 1) * wide]
            for p in range(wide // cap):
                out[k, :, c * (wide // cap) + p, :] = jnp.where(keep, total[:, p * cap:(p + 1) * cap], 0.0)

    def drain(c):
        for k in range(2):
            ring_copy(0, k, k, c).wait_send()
            for way in range(2):
                each(half - 1, lambda step: ring_copy(step + 1, way, k, c).wait_send())

    each(pieces, drain)
    each(blocks, lambda cb: [halo_block(side, cb).wait_send() for side in (0, 1)])


def body(theta, block_dims, pair_mask, term_charge, left_env, right_env, site_one, site_two):
    sectors, cap, pairs, _ = theta.shape
    terms = left_env.shape[0]
    half = lax.axis_size("mpo") // 2
    rc = cap // (2 * half)
    anywhere = pl.BlockSpec(memory_space=pl.ANY)
    vmem = pl.BlockSpec(memory_space=pltpu.VMEM)
    smem = pl.BlockSpec(memory_space=pltpu.SMEM)
    return pl.pallas_call(
        kernel,
        out_shape=jax.ShapeDtypeStruct((sectors, rc, pairs, cap), F32),
        in_specs=[anywhere] * 3 + [smem] * 5,
        out_specs=vmem,
        scratch_shapes=[
            pltpu.VMEM((sectors, cap * pairs, cap), F32),
            pltpu.VMEM((2, cap * pairs, cap), F32),
            pltpu.VMEM(left_env.shape, F32),
            pltpu.VMEM(right_env.shape, F32),
            pltpu.VMEM((2, 8, cap), F32),
            pltpu.VMEM((2, 8, cap), F32),
            pltpu.VMEM((4, 8, cap), F32),
            pltpu.VMEM((4, cap // CB, pairs * CB, 2 * cap), BF16),
            pltpu.VMEM((2 * terms, 2 * cap, 2 * cap), BF16),
            pltpu.VMEM((2 * terms, 2 * cap, pairs * cap), BF16),
            pltpu.VMEM((half, 2, terms, 4 * rc, 2 * cap), BF16),
            pltpu.VMEM((half, 2, 2, rc, pairs * cap), F32),
            pltpu.VMEM((half, 2, 2, rc, pairs * cap), F32),
            pltpu.SemaphoreType.DMA((3,)),
            pltpu.SemaphoreType.DMA((cap // CB + 1, 2)),
            pltpu.SemaphoreType.DMA((cap // CB + 1, 2)),
            pltpu.SemaphoreType.DMA((half, 2, 2, pairs * cap // WIDE)),
            pltpu.SemaphoreType.DMA((half, 2, 2, pairs * cap // WIDE)),
        ],
        compiler_params=pltpu.CompilerParams(
            collective_id=0, has_side_effects=True, vmem_limit_bytes=60 * 2**20
        ),
    )(
        theta.reshape(sectors, cap * pairs, cap), left_env, right_env, block_dims, term_charge,
        pair_mask.T, jnp.transpose(site_one, (1, 2, 0)), jnp.transpose(site_two, (1, 2, 0)),
    )


def solution(mesh):
    placed = (
        P("blk", None, None, None),
        P("blk", None),
        P(None, "blk"),
        P(),
        P("mpo", "blk", None, None),
        P("mpo", "blk", None, None),
        P(),
        P(),
    )
    return jax.shard_map(
        body, mesh=mesh, in_specs=placed, out_specs=P("blk", "mpo", None, None), check_vma=False
    )
```
